128 devices in a mesh: blk: 16 (over y, x_hi, core), rep: 8 (over x_lo, z).
Axes of the slice: x: 4 (x_hi: 2, x_lo: 2; x = x_hi * 2 + x_lo), y: 4, z: 4, core: 2. Of those that a mesh axis runs over, the one named last changes fastest.
Arguments:
- cotangent: bfloat16 [512, 256, 128], P('blk', 'rep'), may hold values from -6 to 6
- relu_mask: int32 [512, 256, 128], P('blk', 'rep'), may hold values 0 or 1
- aggregated: bfloat16 [512, 256, 128], P('blk', 'rep'), may hold values from -6 to 6
- weight: bfloat16 [256, 256], P('rep'), may hold values from -0.375 to 0.375
- tiles: bfloat16 [512, 16, 128, 128], P('blk'), may hold values from -0.125 to 0.125
- col_block: int32 [512, 16], P('blk'), may hold values from 0 to 511, as said below
- live_count: int32 [512], P('blk'), may hold values from 1 to 16, as said below
Outputs:
- input_grad: bfloat16 [512, 256, 128], P('blk', 'rep')
- weight_grad: float32 [256, 256], P('rep')
The draws below stay inside these ranges and needn't reach their ends.
Inputs may be any that keep to these rules, and one draw needn't show every extreme that they name: The slab of a row block b is b // 32; the slab of col_block[b, s] lies at most 2 slabs from it around the closed cycle of the 16 slabs, and both distance 2 directions occur. `live_count`: row blocks of one slab share a density level, so live counts differ from slab to slab; some row block has all 16 slots live.
All inputs are finite; a program needn't handle non-finite values. No bound on the sum of `relu_mask` on one device may be relied on, other than what follows from the above.
Results may differ from the reference program's by a relative error of at most 0.0049.
Values may be sent and summed in bfloat16 or wider, within the bound.
A program may use at most 128 MiB of HBM per device.

```python
import math
import jax
import jax.numpy as jnp
from jax import lax

WIDTH = 256
TILE = 128
SLOTS = 16
REACH = 2
BLOCKS_DEV = 32
BLOCKS = 512
NODES = 65536


def draw_col_block(key, part):
    slabs = BLOCKS // BLOCKS_DEV
    key_off = jax.random.fold_in(key, 11)
    key_in = jax.random.fold_in(key, 12)
    offsets = jax.random.randint(key_off, (BLOCKS, SLOTS), -REACH, REACH + 1, dtype=jnp.int32)
    offsets = offsets.at[0, 0].set(REACH)
    offsets = offsets.at[0, 1].set(-REACH)
    within = jax.random.randint(key_in, (BLOCKS, SLOTS), 0, BLOCKS_DEV, dtype=jnp.int32)
    row_slab = (jnp.arange(BLOCKS, dtype=jnp.int32) // BLOCKS_DEV)[:, None]
    target = (row_slab + offsets) % slabs * BLOCKS_DEV + within
    return target.astype(jnp.int32)


def draw_live_count(key, part):
    slabs = BLOCKS // BLOCKS_DEV
    key_level = jax.random.fold_in(key, 21)
    key_each = jax.random.fold_in(key, 22)
    level = jax.random.randint(key_level, (slabs,), max(1, SLOTS // 4), SLOTS + 1, dtype=jnp.int32)
    level = jnp.repeat(level, BLOCKS_DEV)
    lowest = jnp.maximum(level // 2, 1)
    spread = jax.random.randint(key_each, (BLOCKS,), 0, 1 << 20, dtype=jnp.int32)
    counts = lowest + spread % (level - lowest + 1)
    counts = counts.at[0].set(SLOTS)
    return counts.astype(jnp.int32)


def plant(values, stream_key, smallest, top_value):
    longest = values.shape.index(max(values.shape))
    spots = []
    for shift in (0, 1):
        where = [jax.random.randint(jax.random.fold_in(stream_key, axis), (), 0, length) for axis, length in enumerate(values.shape)]
        where[longest] = (where[longest] + shift) % values.shape[longest]
        spots.append(tuple(where))
    return values.at[spots[0]].set(smallest).at[spots[1]].set(top_value)


def steps_of(stream_key, dims, split, smallest, largest):
    def one(dim, shards_of):
        steps = jax.random.uniform(jax.random.fold_in(jax.random.fold_in(stream_key, 6), dim), (shards_of,), jnp.float32, smallest / len(split), largest / len(split))
        return jnp.repeat(jnp.exp(steps), dims[dim] // shards_of).reshape((-1,) + (1,) * (len(dims) - dim - 1))

    loudness = one(*split[0])
    for cut in split[1:]:
        loudness = loudness * one(*cut)
    return loudness


def centred(own_key, extent, width, reach, pieces=(), kind=jnp.bfloat16):
    gain = steps_of(own_key, extent, pieces, -0.22, 0.18) if pieces else 1.0
    values = jax.random.normal(own_key, extent, jnp.float32) * width * gain
    return jnp.minimum(jnp.maximum(values, -reach), reach).astype(kind)


def setup_inputs(seed: int = 0) -> dict:
    key_list = jax.random.split(jax.random.key(seed), 8)
    return {
        "cotangent": centred(key_list[0], (BLOCKS, WIDTH, TILE), 1.0, 6.0, ((0, 16), (1, 8))),
        "relu_mask": plant((jax.random.randint(key_list[1], (BLOCKS, WIDTH, TILE), 0, 2) < 1).astype(jnp.int32), jax.random.fold_in(key_list[1], 1), 0, 1),
        "aggregated": centred(key_list[2], (BLOCKS, WIDTH, TILE), 1.0, 6.0, ((0, 16), (1, 8))),
        "weight": centred(key_list[3], (WIDTH, WIDTH), WIDTH ** -0.5, 0.375, ((0, 8),)),
        "tiles": centred(key_list[4], (BLOCKS, SLOTS, TILE, TILE), (TILE * SLOTS) ** -0.5, 0.125, ((0, 16),)),
        "col_block": draw_col_block(jax.random.fold_in(key_list[7], 71), 0),
        "live_count": draw_live_count(jax.random.fold_in(key_list[7], 71), 0),
    }


def reference(cotangent, relu_mask, aggregated, weight, tiles, col_block, live_count):
    grad_z = cotangent * relu_mask.astype(jnp.bfloat16)
    grad_zf = grad_z.astype(jnp.float32)
    grad_h = jnp.einsum('io,bon->bin', weight.astype(jnp.float32), grad_zf).astype(jnp.bfloat16)
    weight_grad = jnp.einsum('bin,bon->io', aggregated.astype(jnp.float32), grad_zf) * (1.0 / math.sqrt(NODES))
    grad_hf = grad_h.astype(jnp.float32)
    slot_tiles = jnp.moveaxis(tiles, 1, 0)
    slot_cols = jnp.transpose(col_block)
    slot_ids = jnp.arange(SLOTS, dtype=jnp.int32)

    def one_slot(total_grad, inputs):
        tile_set, cols, slot_id = inputs
        live = (slot_id < live_count).astype(jnp.float32)
        masked = tile_set.astype(jnp.float32) * live[:, None, None]
        terms = jnp.einsum('bij,bfi->bfj', masked, grad_hf)
        total_grad = total_grad + jax.ops.segment_sum(terms, cols, num_segments=BLOCKS)
        return (total_grad, None)
    start_grad = jnp.zeros((BLOCKS, WIDTH, TILE), jnp.float32)
    input_grad, unused = lax.scan(one_slot, start_grad, (slot_tiles, slot_cols, slot_ids))
    return (input_grad.astype(jnp.bfloat16), weight_grad)
```

```python
import functools
import math

import jax
import jax.numpy as jnp
from jax import lax
from jax.experimental import pallas as pl
from jax.experimental.pallas import tpu as pltpu
from jax.sharding import PartitionSpec as P

REACH = 2
GROUPS = 4
PIECES = 4
MESH = pl.DeviceIdType.MESH
VMEM = pl.BlockSpec(memory_space=pltpu.VMEM)


def gather_kernel(
    ring, cot_ref, mask_ref, agg_ref, w_ref, gh_ref, wpart_ref, held, wacc, send_sem, recv_sem
):
    blocks, cols, _ = cot_ref.shape
    me = lax.axis_index("rep")
    side = me // ring
    place = me % ring

    def rank(xrel, zrel):
        x = side if xrel == 0 else 1 - side
        return x * ring + (place + zrel + ring) % ring

    to = {"x": rank(1, 0), "p": rank(0, 1), "m": rank(0, -1)}
    barrier = pltpu.get_barrier_semaphore()
    for name in ("x", "p", "m"):
        pl.semaphore_signal(barrier, inc=1, device_id={"rep": to[name]}, device_id_type=MESH)
    own = pl.multiple_of(me * cols, cols)
    held[:, pl.ds(own, cols), :] = cot_ref[...] * mask_ref[...].astype(jnp.bfloat16)
    wacc[...] = jnp.zeros_like(wacc)
    pl.semaphore_wait(barrier, 3)

    per = blocks // GROUPS

    def slot(xrel, zrel):
        return (xrel % 2) * ring + zrel % ring

    def copy(g, xrel, zrel, name, k):
        at = pl.multiple_of(rank(xrel, zrel) * cols, cols)
        piece = held.at[pl.ds(g * per, per), pl.ds(at, cols), :]
        there = {"x": (xrel + 1, zrel), "p": (xrel, zrel - 1), "m": (xrel, zrel + 1)}[name]
        return pltpu.make_async_remote_copy(
            src_ref=piece,
            dst_ref=piece,
            send_sem=send_sem.at[g, k],
            recv_sem=recv_sem.at[g, slot(*there)],
            device_id={"rep": to[name]},
            device_id_type=MESH,
        )

    def arrived(g, xrel, zrel):
        at = pl.multiple_of(rank(xrel, zrel) * cols, cols)
        piece = held.at[pl.ds(g * per, per), pl.ds(at, cols), :]
        pltpu.make_async_remote_copy(
            src_ref=piece,
            dst_ref=piece,
            send_sem=send_sem.at[g, 0],
            recv_sem=recv_sem.at[g, slot(xrel, zrel)],
            device_id={"rep": to["x"]},
            device_id_type=MESH,
        ).wait_recv()

    sent = []

    def send(*what):
        sent.append(copy(*what))
        sent[-1].start()

    for g in range(GROUPS):
        send(g, 0, 0, "x", 0)
        send(g, 0, 0, "p", 1)
        send(g, 0, 0, "m", 2)
    for g in range(GROUPS):
        arrived(g, 0, -1)
        arrived(g, 0, 1)
        arrived(g, 1, 0)
        if g % 2 == 0:
            send(g, 0, -1, "x", 3)
            send(g, 0, 1, "x", 4)
            send(g, 0, -1, "p", 5)
        else:
            send(g, 1, 0, "p", 3)
            send(g, 1, 0, "m", 4)
            send(g, 0, 1, "m", 5)
    for g in range(GROUPS):
        arrived(g, 1, -1)
        arrived(g, 1, 1)
        arrived(g, 0, 2)
        if g % 2 == 0:
            send(g, 1, -1, "p", 6)
        else:
            send(g, 1, 1, "m", 6)
    for g in range(GROUPS):
        arrived(g, 1, 2)

        def step(i, carry):
            for j in range(4):
                b = g * per + i * 4 + j
                z = held[b]
                gh_ref[b] = jnp.dot(
                    w_ref[...], z, preferred_element_type=jnp.float32
                ).astype(jnp.bfloat16)
                wacc[...] += lax.dot_general(
                    agg_ref[b], z, (((1,), (1,)), ((), ())), preferred_element_type=jnp.float32
                )
            return carry

        lax.fori_loop(0, per // 4, step, 0)
    wpart_ref[...] = wacc[...]
    for one in sent:
        one.wait_send()


def tile_kernel(slabs, blocks, col_ref, live_ref, gh_ref, tiles_ref, mid_ref, out_ref, acc):
    step = pl.program_id(0)
    per, slots = tiles_ref.shape[0], tiles_ref.shape[1]
    window = (2 * REACH + 1) * blocks
    slab = lax.axis_index("blk")

    @pl.when(step == 0)
    def _():
        acc[...] = jnp.zeros_like(acc)

    for k in range(per):
        b = step * per + k
        live = live_ref[b]
        grad = gh_ref[b]
        for first in range(0, slots, 4):

            @pl.when(first < live)
            def _(first=first, k=k, b=b, live=live, grad=grad):
                for s in range(first, first + 4):
                    col = col_ref[b, s]
                    away = (col // blocks - slab + (REACH + slabs)) % slabs
                    row = jnp.where(s < live, away * blocks + col % blocks, window)
                    term = jnp.dot(grad, tiles_ref[k, s], preferred_element_type=jnp.float32)
                    acc[row] += term

    @pl.when(step == pl.num_programs(0) - 1)
    def _():
        for w in range(2 * REACH + 1):
            part = acc[w * blocks : (w + 1) * blocks]
            if w == REACH:
                mid_ref[...] = part
            else:
                out_ref[w - (w > REACH)] = part.astype(jnp.bfloat16)


def exchange_kernel(
    slabs, scale, mid_ref, out_ref, wpart_ref, ig_ref, wg_ref,
    near_in, far_in, both, both_in, far_here, wsum, wsum_in, sems_s, sems_r,
):
    blocks = mid_ref.shape[0]
    per = blocks // PIECES
    me = lax.axis_index("blk")
    core = me % 2
    ahead = 2 * core - 1

    def at(offset):
        return (me + offset + slabs) % slabs

    def across(bit):
        return me + bit - 2 * bit * ((me // bit) % 2)

    bits = [1] + [bit for bit in (4, 8) if bit < slabs] + [2]
    partner = across(1)
    peers = [at(ahead), at(2 * ahead), at(-2 * ahead)] + [across(bit) for bit in bits]
    barrier = pltpu.get_barrier_semaphore()
    for peer in peers:
        pl.semaphore_signal(barrier, inc=1, device_id={"blk": peer}, device_id_type=MESH)
    pl.semaphore_wait(barrier, len(peers))

    far, near = 3 * core, 1 + core
    back_far, back_near = 3 - 3 * core, 2 - core

    def copy(src, dst, k, peer):
        return pltpu.make_async_remote_copy(
            src_ref=src,
            dst_ref=dst,
            send_sem=sems_s.at[k],
            recv_sem=sems_r.at[k],
            device_id={"blk": peer},
            device_id_type=MESH,
        )

    cuts = [pl.ds(p * per, per) for p in range(PIECES)]
    helps = [copy(out_ref.at[back_far, c], far_here.at[c], p, partner) for p, c in enumerate(cuts)]
    k = PIECES
    summed = [copy(both.at[c], both_in.at[c], k + p, at(ahead)) for p, c in enumerate(cuts)]
    k += PIECES
    far_copy = copy(out_ref.at[far], far_in, k, at(2 * ahead))
    near_copy = copy(out_ref.at[back_near], near_in, k + 1, partner)
    k += 2
    for one in helps:
        one.start()
    far_copy.start()
    near_copy.start()
    weights = []
    for i, bit in enumerate(bits):
        src = wpart_ref if i == 0 else wsum.at[i - 1]
        weights.append(copy(src, wsum_in.at[i], k + i, across(bit)))
    weights[0].start()
    for p, c in enumerate(cuts):
        helps[p].wait_recv()
        both[c] = (
            out_ref[near, c].astype(jnp.float32) + far_here[c].astype(jnp.float32)
        ).astype(jnp.bfloat16)
        summed[p].start()
    for i in range(len(bits)):
        weights[i].wait_recv()
        total = (wpart_ref[...] if i == 0 else wsum[i - 1]) + wsum_in[i]
        if i + 1 < len(bits):
            wsum[i] = total
            weights[i + 1].start()
        else:
            wg_ref[...] = total * scale
    near_copy.wait_recv()
    far_copy.wait_recv()
    for p, c in enumerate(cuts):
        summed[p].wait_recv()
        ig_ref[c] = (
            mid_ref[c]
            + near_in[c].astype(jnp.float32)
            + far_in[c].astype(jnp.float32)
            + both_in[c].astype(jnp.float32)
        ).astype(jnp.bfloat16)
    for one in helps + summed + weights + [far_copy, near_copy]:
        one.wait_send()


def on_device(cotangent, relu_mask, aggregated, weight, tiles, col_block, live_count):
    blocks, cols, size = cotangent.shape
    slots = tiles.shape[1]
    slabs, reps = lax.axis_size("blk"), lax.axis_size("rep")
    width = weight.shape[1]
    ring = reps // 2
    bf16, f32 = jnp.bfloat16, jnp.float32
    dma = pltpu.SemaphoreType.DMA

    grad_h, wpart = pl.pallas_call(
        functools.partial(gather_kernel, ring),
        out_shape=(
            jax.ShapeDtypeStruct((blocks, cols, size), bf16),
            jax.ShapeDtypeStruct((cols, width), f32),
        ),
        in_specs=[VMEM] * 4,
        out_specs=(VMEM, VMEM),
        scratch_shapes=[
            pltpu.VMEM((blocks, width, size), bf16),
            pltpu.VMEM((cols, width), f32),
            dma((GROUPS, 7)),
            dma((GROUPS, reps)),
        ],
        compiler_params=pltpu.CompilerParams(
            collective_id=0, has_side_effects=True, vmem_limit_bytes=32 << 20
        ),
        name="gather",
    )(cotangent, relu_mask, aggregated, weight)

    per = 2
    middle, outer = pl.pallas_call(
        functools.partial(tile_kernel, slabs, blocks),
        out_shape=(
            jax.ShapeDtypeStruct((blocks, cols, size), f32),
            jax.ShapeDtypeStruct((2 * REACH, blocks, cols, size), bf16),
        ),
        grid_spec=pltpu.PrefetchScalarGridSpec(
            num_scalar_prefetch=2,
            grid=(blocks // per,),
            in_specs=[
                pl.BlockSpec((blocks, cols, size), lambda i, c, n: (0, 0, 0)),
                pl.BlockSpec((per, slots, size, size), lambda i, c, n: (i, 0, 0, 0)),
            ],
            out_specs=[
                pl.BlockSpec((blocks, cols, size), lambda i, c, n: (0, 0, 0)),
                pl.BlockSpec((2 * REACH, blocks, cols, size), lambda i, c, n: (0, 0, 0, 0)),
            ],
            scratch_shapes=[pltpu.VMEM(((2 * REACH + 1) * blocks + 1, cols, size), f32)],
        ),
        compiler_params=pltpu.CompilerParams(
            dimension_semantics=("arbitrary",), vmem_limit_bytes=32 << 20
        ),
        name="tiles",
    )(col_block, live_count, grad_h, tiles)

    scale = 1.0 / math.sqrt(slabs * blocks * size)
    levels = slabs.bit_length() - 1
    held = pltpu.VMEM((blocks, cols, size), bf16)
    count = 2 * PIECES + 2 + levels
    return pl.pallas_call(
        functools.partial(exchange_kernel, slabs, scale),
        out_shape=(
            jax.ShapeDtypeStruct((blocks, cols, size), bf16),
            jax.ShapeDtypeStruct((cols, width), f32),
        ),
        in_specs=[VMEM] * 3,
        out_specs=(VMEM, VMEM),
        scratch_shapes=[
            held, held, held, held, held,
            pltpu.VMEM((levels, cols, width), f32),
            pltpu.VMEM((levels, cols, width), f32),
            dma((count,)),
            dma((count,)),
        ],
        compiler_params=pltpu.CompilerParams(
            collective_id=1, has_side_effects=True, vmem_limit_bytes=32 << 20
        ),
        name="exchange",
    )(middle, outer, wpart)


def solution(mesh):
    placed = (
        P("blk", "rep", None),
        P("blk", "rep", None),
        P("blk", "rep", None),
        P("rep", None),
        P("blk", None, None, None),
        P("blk", None),
        P("blk"),
    )
    return jax.shard_map(
        on_device,
        mesh=mesh,
        in_specs=placed,
        out_specs=(P("blk", "rep", None), P("rep", None)),
        check_vma=False,
    )
```

```python
import functools
import math

import jax
import jax.numpy as jnp
from jax import lax
from jax.experimental import pallas as pl
from jax.experimental.pallas import tpu as pltpu
from jax.sharding import PartitionSpec as P

REACH = 2
GROUPS = 4
PIECES = 4
MESH = pl.DeviceIdType.MESH
VMEM = pl.BlockSpec(memory_space=pltpu.VMEM)
SMEM = pl.BlockSpec(memory_space=pltpu.SMEM)
HBM = pl.BlockSpec(memory_space=pltpu.HBM)


def gather_kernel(
    ring, cot_hbm, mask_hbm, agg_hbm, w_hbm, tiles_hbm, gh_ref, wpart_ref, tiles_ref,
    cot_ref, mask_ref, agg_ref, w_ref, held, wacc, load_sem, send_sem, recv_sem,
):
    blocks, cols, _ = cot_ref.shape
    pairs = ((mask_hbm, mask_ref), (cot_hbm, cot_ref), (agg_hbm, agg_ref), (w_hbm, w_ref))
    pairs += ((tiles_hbm, tiles_ref),)
    loads = [pltpu.make_async_copy(a, b, load_sem.at[i]) for i, (a, b) in enumerate(pairs)]
    for one in loads[:4]:
        one.start()
    me = lax.axis_index("rep")
    side = me // ring
    place = me % ring

    def rank(xrel, zrel):
        x = side if xrel == 0 else 1 - side
        return x * ring + (place + zrel + ring) % ring

    to = {"x": rank(1, 0), "p": rank(0, 1), "m": rank(0, -1)}
    barrier = pltpu.get_barrier_semaphore()
    for name in ("x", "p", "m"):
        pl.semaphore_signal(barrier, inc=1, device_id={"rep": to[name]}, device_id_type=MESH)
    own = pl.multiple_of(me * cols, cols)
    loads[0].wait()
    loads[1].wait()
    held[:, pl.ds(own, cols), :] = cot_ref[...] * mask_ref[...].astype(jnp.bfloat16)
    wacc[...] = jnp.zeros_like(wacc)
    pl.semaphore_wait(barrier, 3)

    per = blocks // GROUPS

    def slot(xrel, zrel):
        return (xrel % 2) * ring + zrel % ring

    def copy(g, xrel, zrel, name, k):
        at = pl.multiple_of(rank(xrel, zrel) * cols, cols)
        piece = held.at[pl.ds(g * per, per), pl.ds(at, cols), :]
        there = {"x": (xrel + 1, zrel), "p": (xrel, zrel - 1), "m": (xrel, zrel + 1)}[name]
        return pltpu.make_async_remote_copy(
            src_ref=piece,
            dst_ref=piece,
            send_sem=send_sem.at[g, k],
            recv_sem=recv_sem.at[g, slot(*there)],
            device_id={"rep": to[name]},
            device_id_type=MESH,
        )

    def arrived(g, xrel, zrel):
        at = pl.multiple_of(rank(xrel, zrel) * cols, cols)
        piece = held.at[pl.ds(g * per, per), pl.ds(at, cols), :]
        pltpu.make_async_remote_copy(
            src_ref=piece,
            dst_ref=piece,
            send_sem=send_sem.at[g, 0],
            recv_sem=recv_sem.at[g, slot(xrel, zrel)],
            device_id={"rep": to["x"]},
            device_id_type=MESH,
        ).wait_recv()

    sent = []

    def send(*what):
        sent.append(copy(*what))
        sent[-1].start()

    for g in range(GROUPS):
        send(g, 0, 0, "x", 0)
        send(g, 0, 0, "p", 1)
        send(g, 0, 0, "m", 2)
    loads[4].start()
    loads[2].wait()
    loads[3].wait()
    for g in range(GROUPS):
        arrived(g, 0, -1)
        arrived(g, 0, 1)
        arrived(g, 1, 0)
        if g % 2 == 0:
            send(g, 0, -1, "x", 3)
            send(g, 0, 1, "x", 4)
            send(g, 0, -1, "p", 5)
        else:
            send(g, 1, 0, "p", 3)
            send(g, 1, 0, "m", 4)
            send(g, 0, 1, "m", 5)
    for g in range(GROUPS):
        arrived(g, 1, -1)
        arrived(g, 1, 1)
        arrived(g, 0, 2)
        if g % 2 == 0:
            send(g, 1, -1, "p", 6)
        else:
            send(g, 1, 1, "m", 6)
    for g in range(GROUPS):
        arrived(g, 1, 2)

        def step(i, carry):
            for j in range(4):
                b = g * per + i * 4 + j
                z = held[b]
                gh_ref[b] = jnp.dot(
                    w_ref[...], z, preferred_element_type=jnp.float32
                ).astype(jnp.bfloat16)
                wacc[...] += lax.dot_general(
                    agg_ref[b], z, (((1,), (1,)), ((), ())), preferred_element_type=jnp.float32
                )
            return carry

        lax.fori_loop(0, per // 4, step, 0)
    wpart_ref[...] = wacc[...]
    for one in sent:
        one.wait_send()
    loads[4].wait()


def tile_kernel(slabs, blocks, col_ref, live_ref, gh_ref, tiles_ref, mid_ref, out_ref, acc):
    slots = tiles_ref.shape[1]
    window = (2 * REACH + 1) * blocks
    every = slabs * blocks
    first_row = (lax.axis_index("blk") - REACH) * blocks
    acc[...] = jnp.zeros_like(acc)

    def step(i, carry):
        pair = (2 * i, 2 * i + 1)
        live = [live_ref[b] for b in pair]
        most = jnp.maximum(live[0], live[1])
        for half in range(2):

            @pl.when(half * (slots // 2) < most)
            def _(half=half):
                for k, b in enumerate(pair):
                    grad = gh_ref[b]
                    for s in range(half * (slots // 2), (half + 1) * (slots // 2)):
                        away = (col_ref[s, b] - first_row + every) & (every - 1)
                        row = jnp.where(s < live[k], away, window)
                        acc[row] += jnp.dot(
                            grad, tiles_ref[b, s], preferred_element_type=jnp.float32
                        )

        return carry

    lax.fori_loop(0, blocks // 2, step, 0)
    for w in range(2 * REACH + 1):
        part = acc[w * blocks : (w + 1) * blocks]
        if w == REACH:
            mid_ref[...] = part
        else:
            out_ref[w - (w > REACH)] = part.astype(jnp.bfloat16)


def exchange_kernel(
    slabs, scale, mid_ref, out_ref, wpart_ref, ig_ref, wg_ref,
    near_in, far_in, both, both_in, far_here, wsum, wsum_in, sems_s, sems_r,
):
    blocks = mid_ref.shape[0]
    per = blocks // PIECES
    me = lax.axis_index("blk")
    core = me % 2
    ahead = 2 * core - 1

    def at(offset):
        return (me + offset + slabs) % slabs

    def across(bit):
        return me + bit - 2 * bit * ((me // bit) % 2)

    bits = [1] + [bit for bit in (4, 8) if bit < slabs] + [2]
    partner = across(1)
    peers = [at(ahead), at(2 * ahead), at(-2 * ahead)] + [across(bit) for bit in bits]
    barrier = pltpu.get_barrier_semaphore()
    for peer in peers:
        pl.semaphore_signal(barrier, inc=1, device_id={"blk": peer}, device_id_type=MESH)
    pl.semaphore_wait(barrier, len(peers))

    far, near = 3 * core, 1 + core
    back_far, back_near = 3 - 3 * core, 2 - core

    def copy(src, dst, k, peer):
        return pltpu.make_async_remote_copy(
            src_ref=src,
            dst_ref=dst,
            send_sem=sems_s.at[k],
            recv_sem=sems_r.at[k],
            device_id={"blk": peer},
            device_id_type=MESH,
        )

    cuts = [pl.ds(p * per, per) for p in range(PIECES)]
    helps = [copy(out_ref.at[back_far, c], far_here.at[c], p, partner) for p, c in enumerate(cuts)]
    k = PIECES
    summed = [copy(both.at[c], both_in.at[c], k + p, at(ahead)) for p, c in enumerate(cuts)]
    k += PIECES
    far_copy = copy(out_ref.at[far], far_in, k, at(2 * ahead))
    near_copy = copy(out_ref.at[back_near], near_in, k + 1, partner)
    k += 2
    for one in helps:
        one.start()
    far_copy.start()
    near_copy.start()
    weights = []
    for i, bit in enumerate(bits):
        src = wpart_ref if i == 0 else wsum.at[i - 1]
        weights.append(copy(src, wsum_in.at[i], k + i, across(bit)))
    weights[0].start()
    for p, c in enumerate(cuts):
        helps[p].wait_recv()
        both[c] = (
            out_ref[near, c].astype(jnp.float32) + far_here[c].astype(jnp.float32)
        ).astype(jnp.bfloat16)
        summed[p].start()
    for i in range(len(bits)):
        weights[i].wait_recv()
        total = (wpart_ref[...] if i == 0 else wsum[i - 1]) + wsum_in[i]
        if i + 1 < len(bits):
            wsum[i] = total
            weights[i + 1].start()
        else:
            wg_ref[...] = total * scale
    near_copy.wait_recv()
    far_copy.wait_recv()
    for p, c in enumerate(cuts):
        summed[p].wait_recv()
        ig_ref[c] = (
            mid_ref[c]
            + near_in[c].astype(jnp.float32)
            + far_in[c].astype(jnp.float32)
            + both_in[c].astype(jnp.float32)
        ).astype(jnp.bfloat16)
    for one in helps + summed + weights + [far_copy, near_copy]:
        one.wait_send()


def on_device(cotangent, relu_mask, aggregated, weight, tiles, col_block, live_count):
    blocks, cols, size = cotangent.shape
    slots = tiles.shape[1]
    slabs, reps = lax.axis_size("blk"), lax.axis_size("rep")
    width = weight.shape[1]
    ring = reps // 2
    bf16, f32 = jnp.bfloat16, jnp.float32
    dma = pltpu.SemaphoreType.DMA

    grad_h, wpart, tiles_here = pl.pallas_call(
        functools.partial(gather_kernel, ring),
        out_shape=(
            jax.ShapeDtypeStruct((blocks, cols, size), bf16),
            jax.ShapeDtypeStruct((cols, width), f32),
            jax.ShapeDtypeStruct(tiles.shape, bf16),
        ),
        in_specs=[HBM] * 5,
        out_specs=(VMEM, VMEM, VMEM),
        scratch_shapes=[
            pltpu.VMEM((blocks, cols, size), bf16),
            pltpu.VMEM((blocks, cols, size), jnp.int32),
            pltpu.VMEM((blocks, cols, size), bf16),
            pltpu.VMEM((cols, width), bf16),
            pltpu.VMEM((blocks, width, size), bf16),
            pltpu.VMEM((cols, width), f32),
            dma((5,)),
            dma((GROUPS, 7)),
            dma((GROUPS, reps)),
        ],
        compiler_params=pltpu.CompilerParams(
            collective_id=0, has_side_effects=True, vmem_limit_bytes=32 << 20
        ),
        name="gather",
    )(*[pltpu.with_memory_space_constraint(a, pltpu.HBM) for a in (cotangent, relu_mask, aggregated, weight)], tiles)

    middle, outer = pl.pallas_call(
        functools.partial(tile_kernel, slabs, blocks),
        out_shape=(
            jax.ShapeDtypeStruct((blocks, cols, size), f32),
            jax.ShapeDtypeStruct((2 * REACH, blocks, cols, size), bf16),
        ),
        in_specs=[SMEM, SMEM, VMEM, VMEM],
        out_specs=(VMEM, VMEM),
        scratch_shapes=[pltpu.VMEM(((2 * REACH + 1) * blocks + 1, cols, size), f32)],
        compiler_params=pltpu.CompilerParams(vmem_limit_bytes=12 << 20),
        name="tiles",
    )(col_block.T, live_count, grad_h, tiles_here)

    scale = 1.0 / math.sqrt(slabs * blocks * size)
    levels = slabs.bit_length() - 1
    held = pltpu.VMEM((blocks, cols, size), bf16)
    count = 2 * PIECES + 2 + levels
    return pl.pallas_call(
        functools.partial(exchange_kernel, slabs, scale),
        out_shape=(
            jax.ShapeDtypeStruct((blocks, cols, size), bf16),
            jax.ShapeDtypeStruct((cols, width), f32),
        ),
        in_specs=[VMEM] * 3,
        out_specs=(VMEM, VMEM),
        scratch_shapes=[
            held, held, held, held, held,
            pltpu.VMEM((levels, cols, width), f32),
            pltpu.VMEM((levels, cols, width), f32),
            dma((count,)),
            dma((count,)),
        ],
        compiler_params=pltpu.CompilerParams(
            collective_id=1, has_side_effects=True, vmem_limit_bytes=32 << 20
        ),
        name="exchange",
    )(middle, outer, wpart)


def solution(mesh):
    placed = (
        P("blk", "rep", None),
        P("blk", "rep", None),
        P("blk", "rep", None),
        P("rep", None),
        P("blk", None, None, None),
        P("blk", None),
        P("blk"),
    )
    return jax.shard_map(
        on_device,
        mesh=mesh,
        in_specs=placed,
        out_specs=(P("blk", "rep", None), P("rep", None)),
        check_vma=False,
    )
```

```python
import functools
import math

import jax
import jax.numpy as jnp
from jax import lax
from jax.experimental import pallas as pl
from jax.experimental.pallas import tpu as pltpu
from jax.sharding import PartitionSpec as P

REACH = 2
GROUPS = 8
PIECES = 4
MESH = pl.DeviceIdType.MESH
VMEM = pl.BlockSpec(memory_space=pltpu.VMEM)
SMEM = pl.BlockSpec(memory_space=pltpu.SMEM)
HBM = pl.BlockSpec(memory_space=pltpu.HBM)


def gather_kernel(
    ring, cot_hbm, mask_hbm, agg_hbm, w_hbm, tiles_hbm, gh_ref, wpart_ref, tiles_ref,
    cot_ref, mask_ref, agg_ref, w_ref, held, wacc, load_sem, send_sem, recv_sem,
):
    blocks, cols, _ = cot_ref.shape
    pairs = ((mask_hbm, mask_ref), (cot_hbm, cot_ref), (agg_hbm, agg_ref), (w_hbm, w_ref))
    pairs += ((tiles_hbm, tiles_ref),)
    loads = [pltpu.make_async_copy(a, b, load_sem.at[i]) for i, (a, b) in enumerate(pairs)]
    for one in loads[:4]:
        one.start()
    me = lax.axis_index("rep")
    side = me // ring
    place = me % ring

    def rank(xrel, zrel):
        x = side if xrel == 0 else 1 - side
        return x * ring + (place + zrel + ring) % ring

    to = {"x": rank(1, 0), "p": rank(0, 1), "m": rank(0, -1)}
    barrier = pltpu.get_barrier_semaphore()
    for name in ("x", "p", "m"):
        pl.semaphore_signal(barrier, inc=1, device_id={"rep": to[name]}, device_id_type=MESH)
    own = pl.multiple_of(me * cols, cols)
    loads[0].wait()
    loads[1].wait()
    held[:, pl.ds(own, cols), :] = cot_ref[...] * mask_ref[...].astype(jnp.bfloat16)
    wacc[...] = jnp.zeros_like(wacc)
    pl.semaphore_wait(barrier, 3)

    per = blocks // GROUPS

    def slot(xrel, zrel):
        return (xrel % 2) * ring + zrel % ring

    def copy(g, xrel, zrel, name, k):
        at = pl.multiple_of(rank(xrel, zrel) * cols, cols)
        piece = held.at[pl.ds(g * per, per), pl.ds(at, cols), :]
        there = {"x": (xrel + 1, zrel), "p": (xrel, zrel - 1), "m": (xrel, zrel + 1)}[name]
        return pltpu.make_async_remote_copy(
            src_ref=piece,
            dst_ref=piece,
            send_sem=send_sem.at[g, k],
            recv_sem=recv_sem.at[g, slot(*there)],
            device_id={"rep": to[name]},
            device_id_type=MESH,
        )

    def arrived(g, xrel, zrel):
        at = pl.multiple_of(rank(xrel, zrel) * cols, cols)
        piece = held.at[pl.ds(g * per, per), pl.ds(at, cols), :]
        pltpu.make_async_remote_copy(
            src_ref=piece,
            dst_ref=piece,
            send_sem=send_sem.at[g, 0],
            recv_sem=recv_sem.at[g, slot(xrel, zrel)],
            device_id={"rep": to["x"]},
            device_id_type=MESH,
        ).wait_recv()

    sent = []

    def send(*what):
        sent.append(copy(*what))
        sent[-1].start()

    for g in range(GROUPS):
        send(g, 0, 0, "x", 0)
        send(g, 0, 0, "p", 1)
        send(g, 0, 0, "m", 2)
    loads[4].start()
    loads[2].wait()
    loads[3].wait()
    for g in range(GROUPS):
        arrived(g, 0, -1)
        arrived(g, 0, 1)
        arrived(g, 1, 0)
        if g % 2 == 0:
            send(g, 0, -1, "x", 3)
            send(g, 0, 1, "x", 4)
            send(g, 0, -1, "p", 5)
        else:
            send(g, 1, 0, "p", 3)
            send(g, 1, 0, "m", 4)
            send(g, 0, 1, "m", 5)
    for g in range(GROUPS):
        arrived(g, 1, -1)
        arrived(g, 1, 1)
        arrived(g, 0, 2)
        if g in (2, 5):
            send(g, 0, 2, "x", 6)
        elif g % 2 == 0:
            send(g, 1, -1, "p", 6)
        else:
            send(g, 1, 1, "m", 6)
    for g in range(GROUPS):
        arrived(g, 1, 2)

        def step(i, carry):
            for j in range(4):
                b = g * per + i * 4 + j
                z = held[b]
                gh_ref[b] = jnp.dot(
                    w_ref[...], z, preferred_element_type=jnp.float32
                ).astype(jnp.bfloat16)
                wacc[...] += lax.dot_general(
                    agg_ref[b], z, (((1,), (1,)), ((), ())), preferred_element_type=jnp.float32
                )
            return carry

        lax.fori_loop(0, per // 4, step, 0)
    wpart_ref[...] = wacc[...]
    for one in sent:
        one.wait_send()
    loads[4].wait()


def tile_kernel(slabs, blocks, col_ref, live_ref, gh_ref, tiles_ref, mid_ref, out_ref, acc, term, rows):
    slots = tiles_ref.shape[1]
    window = (2 * REACH + 1) * blocks
    every = slabs * blocks
    first_row = (lax.axis_index("blk") - REACH) * blocks
    acc[...] = jnp.zeros_like(acc)
    term[...] = jnp.zeros_like(term)
    count = term.shape[0]
    for t in range(count):
        rows[t] = window

    def settle():
        for t in range(count):
            acc[rows[t]] += term[t]

    def step(i, carry):
        pair = (2 * i, 2 * i + 1)
        live = [live_ref[b] for b in pair]
        most = jnp.maximum(live[0], live[1])
        for half in range(2):

            @pl.when(half * (slots // 2) < most)
            def _(half=half):
                settle()
                t = 0
                for k, b in enumerate(pair):
                    grad = gh_ref[b]
                    for s in range(half * (slots // 2), (half + 1) * (slots // 2)):
                        away = (col_ref[s, b] - first_row + every) & (every - 1)
                        rows[t] = jnp.where(s < live[k], away, window)
                        term[t] = jnp.dot(
                            grad, tiles_ref[b, s], preferred_element_type=jnp.float32
                        )
                        t += 1

        return carry

    lax.fori_loop(0, blocks // 2, step, 0)
    settle()
    for w in range(2 * REACH + 1):
        part = acc[w * blocks : (w + 1) * blocks]
        if w == REACH:
            mid_ref[...] = part
        else:
            out_ref[w - (w > REACH)] = part.astype(jnp.bfloat16)


def exchange_kernel(
    slabs, scale, mid_ref, out_ref, wpart_ref, ig_ref, wg_ref,
    near_in, far_in, both, both_in, far_here, wsum, wsum_in, sems_s, sems_r,
):
    blocks = mid_ref.shape[0]
    per = blocks // PIECES
    me = lax.axis_index("blk")
    core = me % 2
    ahead = 2 * core - 1

    def at(offset):
        return (me + offset + slabs) % slabs

    def across(bit):
        return me + bit - 2 * bit * ((me // bit) % 2)

    bits = [2, 1] + [bit for bit in (4, 8) if bit < slabs]
    partner = across(1)
    peers = [at(ahead), at(2 * ahead), at(-2 * ahead)] + [across(bit) for bit in bits]
    barrier = pltpu.get_barrier_semaphore()
    for peer in peers:
        pl.semaphore_signal(barrier, inc=1, device_id={"blk": peer}, device_id_type=MESH)
    pl.semaphore_wait(barrier, len(peers))

    far, near = 3 * core, 1 + core
    back_far, back_near = 3 - 3 * core, 2 - core

    def copy(src, dst, k, peer):
        return pltpu.make_async_remote_copy(
            src_ref=src,
            dst_ref=dst,
            send_sem=sems_s.at[k],
            recv_sem=sems_r.at[k],
            device_id={"blk": peer},
            device_id_type=MESH,
        )

    cuts = [pl.ds(p * per, per) for p in range(PIECES)]
    helps = [copy(out_ref.at[back_far, c], far_here.at[c], p, partner) for p, c in enumerate(cuts)]
    k = PIECES
    summed = [copy(both.at[c], both_in.at[c], k + p, at(ahead)) for p, c in enumerate(cuts)]
    k += PIECES
    far_copy = copy(out_ref.at[far], far_in, k, at(2 * ahead))
    near_copy = copy(out_ref.at[back_near], near_in, k + 1, partner)
    k += 2
    weights = []
    for i, bit in enumerate(bits):
        src = wpart_ref if i == 0 else wsum.at[i - 1]
        weights.append(copy(src, wsum_in.at[i], k + i, across(bit)))
    weights[0].start()
    for one in helps:
        one.start()
    far_copy.start()
    near_copy.start()
    for p, c in enumerate(cuts):
        helps[p].wait_recv()
        both[c] = (
            out_ref[near, c].astype(jnp.float32) + far_here[c].astype(jnp.float32)
        ).astype(jnp.bfloat16)
        summed[p].start()
    for i in range(len(bits)):
        weights[i].wait_recv()
        total = (wpart_ref[...] if i == 0 else wsum[i - 1]) + wsum_in[i]
        if i + 1 < len(bits):
            wsum[i] = total
            weights[i + 1].start()
        else:
            wg_ref[...] = total * scale
    near_copy.wait_recv()
    far_copy.wait_recv()
    for p, c in enumerate(cuts):
        summed[p].wait_recv()
        ig_ref[c] = (
            mid_ref[c]
            + near_in[c].astype(jnp.float32)
            + far_in[c].astype(jnp.float32)
            + both_in[c].astype(jnp.float32)
        ).astype(jnp.bfloat16)
    for one in helps + summed + weights + [far_copy, near_copy]:
        one.wait_send()


def on_device(cotangent, relu_mask, aggregated, weight, tiles, col_block, live_count):
    blocks, cols, size = cotangent.shape
    slots = tiles.shape[1]
    slabs, reps = lax.axis_size("blk"), lax.axis_size("rep")
    width = weight.shape[1]
    ring = reps // 2
    bf16, f32 = jnp.bfloat16, jnp.float32
    dma = pltpu.SemaphoreType.DMA

    grad_h, wpart, tiles_here = pl.pallas_call(
        functools.partial(gather_kernel, ring),
        out_shape=(
            jax.ShapeDtypeStruct((blocks, cols, size), bf16),
            jax.ShapeDtypeStruct((cols, width), f32),
            jax.ShapeDtypeStruct(tiles.shape, bf16),
        ),
        in_specs=[HBM] * 5,
        out_specs=(VMEM, VMEM, VMEM),
        scratch_shapes=[
            pltpu.VMEM((blocks, cols, size), bf16),
            pltpu.VMEM((blocks, cols, size), jnp.int32),
            pltpu.VMEM((blocks, cols, size), bf16),
            pltpu.VMEM((cols, width), bf16),
            pltpu.VMEM((blocks, width, size), bf16),
            pltpu.VMEM((cols, width), f32),
            dma((5,)),
            dma((GROUPS, 7)),
            dma((GROUPS, reps)),
        ],
        compiler_params=pltpu.CompilerParams(
            collective_id=0, has_side_effects=True, vmem_limit_bytes=32 << 20
        ),
        name="gather",
    )(*[pltpu.with_memory_space_constraint(a, pltpu.HBM) for a in (cotangent, relu_mask, aggregated, weight)], tiles)

    middle, outer = pl.pallas_call(
        functools.partial(tile_kernel, slabs, blocks),
        out_shape=(
            jax.ShapeDtypeStruct((blocks, cols, size), f32),
            jax.ShapeDtypeStruct((2 * REACH, blocks, cols, size), bf16),
        ),
        in_specs=[SMEM, SMEM, VMEM, VMEM],
        out_specs=(VMEM, VMEM),
        scratch_shapes=[
            pltpu.VMEM(((2 * REACH + 1) * blocks + 1, cols, size), f32),
            pltpu.VMEM((slots, cols, size), f32),
            pltpu.SMEM((slots,), jnp.int32),
        ],
        compiler_params=pltpu.CompilerParams(vmem_limit_bytes=12 << 20),
        name="tiles",
    )(col_block.T, live_count, grad_h, tiles_here)

    scale = 1.0 / math.sqrt(slabs * blocks * size)
    levels = slabs.bit_length() - 1
    held = pltpu.VMEM((blocks, cols, size), bf16)
    count = 2 * PIECES + 2 + levels
    return pl.pallas_call(
        functools.partial(exchange_kernel, slabs, scale),
        out_shape=(
            jax.ShapeDtypeStruct((blocks, cols, size), bf16),
            jax.ShapeDtypeStruct((cols, width), f32),
        ),
        in_specs=[VMEM] * 3,
        out_specs=(VMEM, VMEM),
        scratch_shapes=[
            held, held, held, held, held,
            pltpu.VMEM((levels, cols, width), f32),
            pltpu.VMEM((levels, cols, width), f32),
            dma((count,)),
            dma((count,)),
        ],
        compiler_params=pltpu.CompilerParams(
            collective_id=1, has_side_effects=True, vmem_limit_bytes=32 << 20
        ),
        name="exchange",
    )(middle, outer, wpart)


def solution(mesh):
    placed = (
        P("blk", "rep", None),
        P("blk", "rep", None),
        P("blk", "rep", None),
        P("rep", None),
        P("blk", None, None, None),
        P("blk", None),
        P("blk"),
    )
    return jax.shard_map(
        on_device,
        mesh=mesh,
        in_specs=placed,
        out_specs=(P("blk", "rep", None), P("rep", None)),
        check_vma=False,
    )
```

```python
import functools
import math

import jax
import jax.numpy as jnp
from jax import lax
from jax.experimental import pallas as pl
from jax.experimental.pallas import tpu as pltpu
from jax.sharding import PartitionSpec as P

REACH = 2
GROUPS = 8
PIECES = 4
MESH = pl.DeviceIdType.MESH
VMEM = pl.BlockSpec(memory_space=pltpu.VMEM)
SMEM = pl.BlockSpec(memory_space=pltpu.SMEM)
HBM = pl.BlockSpec(memory_space=pltpu.HBM)


def gather_kernel(
    ring, cot_hbm, mask_hbm, agg_hbm, w_hbm, tiles_hbm, gh_ref, wpart_ref, tiles_ref,
    cot_ref, mask_ref, agg_ref, w_ref, held, wacc, load_sem, send_sem, recv_sem,
):
    blocks, cols, _ = cot_ref.shape
    pairs = ((mask_hbm, mask_ref), (cot_hbm, cot_ref), (agg_hbm, agg_ref), (w_hbm, w_ref))
    pairs += ((tiles_hbm, tiles_ref),)
    loads = [pltpu.make_async_copy(a, b, load_sem.at[i]) for i, (a, b) in enumerate(pairs)]
    for one in loads[:4]:
        one.start()
    me = lax.axis_index("rep")
    side = me // ring
    place = me % ring

    def rank(xrel, zrel):
        x = side if xrel == 0 else 1 - side
        return x * ring + (place + zrel + ring) % ring

    to = {"x": rank(1, 0), "p": rank(0, 1), "m": rank(0, -1)}
    barrier = pltpu.get_barrier_semaphore()
    for name in ("x", "p", "m"):
        pl.semaphore_signal(barrier, inc=1, device_id={"rep": to[name]}, device_id_type=MESH)
    own = pl.multiple_of(me * cols, cols)
    loads[0].wait()
    loads[1].wait()
    held[:, pl.ds(own, cols), :] = cot_ref[...] * mask_ref[...].astype(jnp.bfloat16)
    wacc[...] = jnp.zeros_like(wacc)
    pl.semaphore_wait(barrier, 3)

    per = blocks // GROUPS

    def slot(xrel, zrel):
        return (xrel % 2) * ring + zrel % ring

    def copy(g, xrel, zrel, name, k):
        at = pl.multiple_of(rank(xrel, zrel) * cols, cols)
        piece = held.at[pl.ds(g * per, per), pl.ds(at, cols), :]
        there = {"x": (xrel + 1, zrel), "p": (xrel, zrel - 1), "m": (xrel, zrel + 1)}[name]
        return pltpu.make_async_remote_copy(
            src_ref=piece,
            dst_ref=piece,
            send_sem=send_sem.at[g, k],
            recv_sem=recv_sem.at[g, slot(*there)],
            device_id={"rep": to[name]},
            device_id_type=MESH,
        )

    def arrived(g, xrel, zrel):
        at = pl.multiple_of(rank(xrel, zrel) * cols, cols)
        piece = held.at[pl.ds(g * per, per), pl.ds(at, cols), :]
        pltpu.make_async_remote_copy(
            src_ref=piece,
            dst_ref=piece,
            send_sem=send_sem.at[g, 0],
            recv_sem=recv_sem.at[g, slot(xrel, zrel)],
            device_id={"rep": to["x"]},
            device_id_type=MESH,
        ).wait_recv()

    sent = []

    def send(*what):
        sent.append(copy(*what))
        sent[-1].start()

    for g in range(GROUPS):
        send(g, 0, 0, "x", 0)
        send(g, 0, 0, "p", 1)
        send(g, 0, 0, "m", 2)
    loads[4].start()
    loads[2].wait()
    loads[3].wait()
    for g in range(GROUPS):
        arrived(g, 0, -1)
        arrived(g, 0, 1)
        arrived(g, 1, 0)
        if g % 2 == 0:
            send(g, 0, -1, "x", 3)
            send(g, 0, 1, "x", 4)
            send(g, 0, -1, "p", 5)
        else:
            send(g, 1, 0, "p", 3)
            send(g, 1, 0, "m", 4)
            send(g, 0, 1, "m", 5)
    for g in range(GROUPS):
        arrived(g, 1, -1)
        arrived(g, 1, 1)
        arrived(g, 0, 2)
        if g in (2, 5):
            send(g, 0, 2, "x", 6)
        elif g % 2 == 0:
            send(g, 1, -1, "p", 6)
        else:
            send(g, 1, 1, "m", 6)
    for g in range(GROUPS):
        arrived(g, 1, 2)

        def step(i, carry):
            for j in range(4):
                b = g * per + i * 4 + j
                z = held[b]
                gh_ref[b] = jnp.dot(
                    w_ref[...], z, preferred_element_type=jnp.float32
                ).astype(jnp.bfloat16)
                wacc[...] += lax.dot_general(
                    agg_ref[b], z, (((1,), (1,)), ((), ())), preferred_element_type=jnp.float32
                )
            return carry

        lax.fori_loop(0, per // 4, step, 0)
    wpart_ref[...] = wacc[...]
    for one in sent:
        one.wait_send()
    loads[4].wait()


def tile_kernel(slabs, blocks, col_ref, live_ref, gh_ref, tiles_ref, mid_ref, out_ref, acc, term, rows):
    slots, size = tiles_ref.shape[1], tiles_ref.shape[3]
    cols = gh_ref.shape[1]
    window = (2 * REACH + 1) * blocks
    every = slabs * blocks
    first_row = (lax.axis_index("blk") - REACH) * blocks
    acc[...] = jnp.zeros_like(acc)
    term[...] = jnp.zeros_like(term)
    count = term.shape[0]
    for t in range(count):
        rows[t] = window

    def settle():
        for t in range(count):
            acc[rows[t]] += term[t]

    def step(i, carry):
        pair = (2 * i, 2 * i + 1)
        live = [live_ref[b] for b in pair]
        most = jnp.maximum(live[0], live[1])
        for half in range(2):

            @pl.when(half * (slots // 2) < most)
            def _(half=half):
                settle()
                t = 0
                for k, b in enumerate(pair):
                    grad = gh_ref[b]
                    for s in range(half * (slots // 2), (half + 1) * (slots // 2), 2):
                        both = jnp.concatenate([tiles_ref[b, s], tiles_ref[b, s + 1]], axis=1)
                        terms = jnp.dot(grad, both, preferred_element_type=jnp.float32)
                        for j in range(2):
                            away = (col_ref[s + j, b] - first_row + every) & (every - 1)
                            rows[t + j] = jnp.where(s + j < live[k], away, window)
                            term[t + j] = terms[:, j * size : (j + 1) * size]
                        t += 2

        return carry

    lax.fori_loop(0, blocks // 2, step, 0)
    settle()
    for w in range(2 * REACH + 1):
        part = acc[w * blocks : (w + 1) * blocks]
        if w == REACH:
            mid_ref[...] = part
        else:
            out_ref[w - (w > REACH)] = part.astype(jnp.bfloat16)


def exchange_kernel(
    slabs, scale, mid_ref, out_ref, wpart_ref, ig_ref, wg_ref,
    near_in, far_in, both, both_in, far_here, wsum, wsum_in, sems_s, sems_r,
):
    blocks = mid_ref.shape[0]
    per = blocks // PIECES
    me = lax.axis_index("blk")
    core = me % 2
    ahead = 2 * core - 1

    def at(offset):
        return (me + offset + slabs) % slabs

    def across(bit):
        return me + bit - 2 * bit * ((me // bit) % 2)

    bits = [2, 1] + [bit for bit in (4, 8) if bit < slabs]
    partner = across(1)
    peers = [at(ahead), at(2 * ahead), at(-2 * ahead)] + [across(bit) for bit in bits]
    barrier = pltpu.get_barrier_semaphore()
    for peer in peers:
        pl.semaphore_signal(barrier, inc=1, device_id={"blk": peer}, device_id_type=MESH)
    pl.semaphore_wait(barrier, len(peers))

    far, near = 3 * core, 1 + core
    back_far, back_near = 3 - 3 * core, 2 - core

    def copy(src, dst, k, peer):
        return pltpu.make_async_remote_copy(
            src_ref=src,
            dst_ref=dst,
            send_sem=sems_s.at[k],
            recv_sem=sems_r.at[k],
            device_id={"blk": peer},
            device_id_type=MESH,
        )

    cuts = [pl.ds(p * per, per) for p in range(PIECES)]
    helps = [copy(out_ref.at[back_far, c], far_here.at[c], p, partner) for p, c in enumerate(cuts)]
    k = PIECES
    summed = [copy(both.at[c], both_in.at[c], k + p, at(ahead)) for p, c in enumerate(cuts)]
    k += PIECES
    far_copy = copy(out_ref.at[far], far_in, k, at(2 * ahead))
    near_copy = copy(out_ref.at[back_near], near_in, k + 1, partner)
    k += 2
    weights = []
    for i, bit in enumerate(bits):
        src = wpart_ref if i == 0 else wsum.at[i - 1]
        weights.append(copy(src, wsum_in.at[i], k + i, across(bit)))
    weights[0].start()
    for one in helps:
        one.start()
    far_copy.start()
    near_copy.start()
    for p, c in enumerate(cuts):
        helps[p].wait_recv()
        both[c] = (
            out_ref[near, c].astype(jnp.float32) + far_here[c].astype(jnp.float32)
        ).astype(jnp.bfloat16)
        summed[p].start()
    for i in range(len(bits)):
        weights[i].wait_recv()
        total = (wpart_ref[...] if i == 0 else wsum[i - 1]) + wsum_in[i]
        if i + 1 < len(bits):
            wsum[i] = total
            weights[i + 1].start()
        else:
            wg_ref[...] = total * scale
    near_copy.wait_recv()
    far_copy.wait_recv()
    for p, c in enumerate(cuts):
        summed[p].wait_recv()
        ig_ref[c] = (
            mid_ref[c]
            + near_in[c].astype(jnp.float32)
            + far_in[c].astype(jnp.float32)
            + both_in[c].astype(jnp.float32)
        ).astype(jnp.bfloat16)
    for one in helps + summed + weights + [far_copy, near_copy]:
        one.wait_send()


def on_device(cotangent, relu_mask, aggregated, weight, tiles, col_block, live_count):
    blocks, cols, size = cotangent.shape
    slots = tiles.shape[1]
    slabs, reps = lax.axis_size("blk"), lax.axis_size("rep")
    width = weight.shape[1]
    ring = reps // 2
    bf16, f32 = jnp.bfloat16, jnp.float32
    dma = pltpu.SemaphoreType.DMA

    grad_h, wpart, tiles_here = pl.pallas_call(
        functools.partial(gather_kernel, ring),
        out_shape=(
            jax.ShapeDtypeStruct((blocks, cols, size), bf16),
            jax.ShapeDtypeStruct((cols, width), f32),
            jax.ShapeDtypeStruct(tiles.shape, bf16),
        ),
        in_specs=[HBM] * 5,
        out_specs=(VMEM, VMEM, VMEM),
        scratch_shapes=[
            pltpu.VMEM((blocks, cols, size), bf16),
            pltpu.VMEM((blocks, cols, size), jnp.int32),
            pltpu.VMEM((blocks, cols, size), bf16),
            pltpu.VMEM((cols, width), bf16),
            pltpu.VMEM((blocks, width, size), bf16),
            pltpu.VMEM((cols, width), f32),
            dma((5,)),
            dma((GROUPS, 7)),
            dma((GROUPS, reps)),
        ],
        compiler_params=pltpu.CompilerParams(
            collective_id=0, has_side_effects=True, vmem_limit_bytes=32 << 20
        ),
        name="gather",
    )(*[pltpu.with_memory_space_constraint(a, pltpu.HBM) for a in (cotangent, relu_mask, aggregated, weight)], tiles)

    middle, outer = pl.pallas_call(
        functools.partial(tile_kernel, slabs, blocks),
        out_shape=(
            jax.ShapeDtypeStruct((blocks, cols, size), f32),
            jax.ShapeDtypeStruct((2 * REACH, blocks, cols, size), bf16),
        ),
        in_specs=[SMEM, SMEM, VMEM, VMEM],
        out_specs=(VMEM, VMEM),
        scratch_shapes=[
            pltpu.VMEM(((2 * REACH + 1) * blocks + 1, cols, size), f32),
            pltpu.VMEM((slots, cols, size), f32),
            pltpu.SMEM((slots,), jnp.int32),
        ],
        compiler_params=pltpu.CompilerParams(vmem_limit_bytes=12 << 20),
        name="tiles",
    )(col_block.T, live_count, grad_h, tiles_here)

    scale = 1.0 / math.sqrt(slabs * blocks * size)
    levels = slabs.bit_length() - 1
    held = pltpu.VMEM((blocks, cols, size), bf16)
    count = 2 * PIECES + 2 + levels
    return pl.pallas_call(
        functools.partial(exchange_kernel, slabs, scale),
        out_shape=(
            jax.ShapeDtypeStruct((blocks, cols, size), bf16),
            jax.ShapeDtypeStruct((cols, width), f32),
        ),
        in_specs=[VMEM] * 3,
        out_specs=(VMEM, VMEM),
        scratch_shapes=[
            held, held, held, held, held,
            pltpu.VMEM((levels, cols, width), f32),
            pltpu.VMEM((levels, cols, width), f32),
            dma((count,)),
            dma((count,)),
        ],
        compiler_params=pltpu.CompilerParams(
            collective_id=1, has_side_effects=True, vmem_limit_bytes=32 << 20
        ),
        name="exchange",
    )(middle, outer, wpart)


def solution(mesh):
    placed = (
        P("blk", "rep", None),
        P("blk", "rep", None),
        P("blk", "rep", None),
        P("rep", None),
        P("blk", None, None, None),
        P("blk", None),
        P("blk"),
    )
    return jax.shard_map(
        on_device,
        mesh=mesh,
        in_specs=placed,
        out_specs=(P("blk", "rep", None), P("rep", None)),
        check_vma=False,
    )
```

```python
import functools
import math

import jax
import jax.numpy as jnp
from jax import lax
from jax.experimental import pallas as pl
from jax.experimental.pallas import tpu as pltpu
from jax.sharding import PartitionSpec as P

REACH = 2
GROUPS = 8
PIECES = 4
MESH = pl.DeviceIdType.MESH
VMEM = pl.BlockSpec(memory_space=pltpu.VMEM)
SMEM = pl.BlockSpec(memory_space=pltpu.SMEM)
HBM = pl.BlockSpec(memory_space=pltpu.HBM)


def gather_kernel(
    ring, cot_hbm, mask_hbm, agg_hbm, w_hbm, tiles_hbm, gh_ref, wpart_ref, tiles_ref,
    cot_ref, mask_ref, agg_ref, w_ref, held, wacc, load_sem, send_sem, recv_sem,
):
    blocks, cols, _ = cot_ref.shape
    pairs = ((mask_hbm, mask_ref), (cot_hbm, cot_ref), (agg_hbm, agg_ref), (w_hbm, w_ref))
    pairs += ((tiles_hbm, tiles_ref),)
    loads = [pltpu.make_async_copy(a, b, load_sem.at[i]) for i, (a, b) in enumerate(pairs)]
    for one in loads[:4]:
        one.start()
    me = lax.axis_index("rep")
    side = me // ring
    place = me % ring

    def rank(xrel, zrel):
        x = side if xrel == 0 else 1 - side
        return x * ring + (place + zrel + ring) % ring

    to = {"x": rank(1, 0), "p": rank(0, 1), "m": rank(0, -1)}
    barrier = pltpu.get_barrier_semaphore()
    for name in ("x", "p", "m"):
        pl.semaphore_signal(barrier, inc=1, device_id={"rep": to[name]}, device_id_type=MESH)
    own = pl.multiple_of(me * cols, cols)
    loads[0].wait()
    loads[1].wait()
    held[:, pl.ds(own, cols), :] = cot_ref[...] * mask_ref[...].astype(jnp.bfloat16)
    wacc[...] = jnp.zeros_like(wacc)
    pl.semaphore_wait(barrier, 3)

    per = blocks // GROUPS

    def slot(xrel, zrel):
        return (xrel % 2) * ring + zrel % ring

    def copy(g, xrel, zrel, name, k):
        at = pl.multiple_of(rank(xrel, zrel) * cols, cols)
        piece = held.at[pl.ds(g * per, per), pl.ds(at, cols), :]
        there = {"x": (xrel + 1, zrel), "p": (xrel, zrel - 1), "m": (xrel, zrel + 1)}[name]
        return pltpu.make_async_remote_copy(
            src_ref=piece,
            dst_ref=piece,
            send_sem=send_sem.at[g, k],
            recv_sem=recv_sem.at[g, slot(*there)],
            device_id={"rep": to[name]},
            device_id_type=MESH,
        )

    def arrived(g, xrel, zrel):
        at = pl.multiple_of(rank(xrel, zrel) * cols, cols)
        piece = held.at[pl.ds(g * per, per), pl.ds(at, cols), :]
        pltpu.make_async_remote_copy(
            src_ref=piece,
            dst_ref=piece,
            send_sem=send_sem.at[g, 0],
            recv_sem=recv_sem.at[g, slot(xrel, zrel)],
            device_id={"rep": to["x"]},
            device_id_type=MESH,
        ).wait_recv()

    sent = []

    def send(*what):
        sent.append(copy(*what))
        sent[-1].start()

    for g in range(GROUPS):
        send(g, 0, 0, "x", 0)
        send(g, 0, 0, "p", 1)
        send(g, 0, 0, "m", 2)
    loads[4].start()
    loads[2].wait()
    loads[3].wait()
    def first(g):
        arrived(g, 0, -1)
        arrived(g, 0, 1)
        arrived(g, 1, 0)
        if g % 2 == 0:
            send(g, 0, -1, "x", 3)
            send(g, 0, 1, "x", 4)
            send(g, 0, -1, "p", 5)
        else:
            send(g, 1, 0, "p", 3)
            send(g, 1, 0, "m", 4)
            send(g, 0, 1, "m", 5)

    def second(g):
        arrived(g, 1, -1)
        arrived(g, 1, 1)
        arrived(g, 0, 2)
        if g in (2, 5):
            send(g, 0, 2, "x", 6)
        elif g % 2 == 0:
            send(g, 1, -1, "p", 6)
        else:
            send(g, 1, 1, "m", 6)

    def finish(g):
        arrived(g, 1, 2)

        def step(i, carry):
            for j in range(4):
                b = g * per + i * 4 + j
                z = held[b]
                gh_ref[b] = jnp.dot(
                    w_ref[...], z, preferred_element_type=jnp.float32
                ).astype(jnp.bfloat16)
                wacc[...] += lax.dot_general(
                    agg_ref[b], z, (((1,), (1,)), ((), ())), preferred_element_type=jnp.float32
                )
            return carry

        lax.fori_loop(0, per // 4, step, 0)

    for t in range(GROUPS + 4):
        for work, late in ((first, 0), (second, 2), (finish, 4)):
            if 0 <= t - late < GROUPS:
                work(t - late)
    wpart_ref[...] = wacc[...]
    for one in sent:
        one.wait_send()
    loads[4].wait()


def tile_kernel(slabs, blocks, col_ref, live_ref, gh_ref, tiles_ref, mid_ref, out_ref, acc, term, rows):
    slots, size = tiles_ref.shape[1], tiles_ref.shape[3]
    cols = gh_ref.shape[1]
    window = (2 * REACH + 1) * blocks
    every = slabs * blocks
    first_row = (lax.axis_index("blk") - REACH) * blocks
    acc[...] = jnp.zeros_like(acc)
    term[...] = jnp.zeros_like(term)
    count = term.shape[0]
    for t in range(count):
        rows[t] = window

    def settle():
        for t in range(count):
            acc[rows[t]] += term[t]

    def step(i, carry):
        pair = (2 * i, 2 * i + 1)
        live = [live_ref[b] for b in pair]
        most = jnp.maximum(live[0], live[1])
        for half in range(2):

            @pl.when(half * (slots // 2) < most)
            def _(half=half):
                settle()
                t = 0
                for k, b in enumerate(pair):
                    grad = gh_ref[b]
                    for s in range(half * (slots // 2), (half + 1) * (slots // 2), 2):
                        both = jnp.concatenate([tiles_ref[b, s], tiles_ref[b, s + 1]], axis=1)
                        terms = jnp.dot(grad, both, preferred_element_type=jnp.float32)
                        for j in range(2):
                            away = (col_ref[s + j, b] - first_row + every) & (every - 1)
                            rows[t + j] = jnp.where(s + j < live[k], away, window)
                            term[t + j] = terms[:, j * size : (j + 1) * size]
                        t += 2

        return carry

    lax.fori_loop(0, blocks // 2, step, 0)
    settle()
    for w in range(2 * REACH + 1):
        part = acc[w * blocks : (w + 1) * blocks]
        if w == REACH:
            mid_ref[...] = part
        else:
            out_ref[w - (w > REACH)] = part.astype(jnp.bfloat16)


def exchange_kernel(
    slabs, scale, mid_ref, out_ref, wpart_ref, ig_ref, wg_ref,
    near_in, far_in, both, both_in, far_here, wsum, wsum_in, sems_s, sems_r,
):
    blocks = mid_ref.shape[0]
    per = blocks // PIECES
    me = lax.axis_index("blk")
    core = me % 2
    ahead = 2 * core - 1

    def at(offset):
        return (me + offset + slabs) % slabs

    def across(bit):
        return me + bit - 2 * bit * ((me // bit) % 2)

    bits = [2, 1] + [bit for bit in (4, 8) if bit < slabs]
    partner = across(1)
    peers = [at(ahead), at(2 * ahead), at(-2 * ahead)] + [across(bit) for bit in bits]
    barrier = pltpu.get_barrier_semaphore()
    for peer in peers:
        pl.semaphore_signal(barrier, inc=1, device_id={"blk": peer}, device_id_type=MESH)
    pl.semaphore_wait(barrier, len(peers))

    far, near = 3 * core, 1 + core
    back_far, back_near = 3 - 3 * core, 2 - core

    def copy(src, dst, k, peer):
        return pltpu.make_async_remote_copy(
            src_ref=src,
            dst_ref=dst,
            send_sem=sems_s.at[k],
            recv_sem=sems_r.at[k],
            device_id={"blk": peer},
            device_id_type=MESH,
        )

    cuts = [pl.ds(p * per, per) for p in range(PIECES)]
    helps = [copy(out_ref.at[back_far, c], far_here.at[c], p, partner) for p, c in enumerate(cuts)]
    k = PIECES
    summed = [copy(both.at[c], both_in.at[c], k + p, at(ahead)) for p, c in enumerate(cuts)]
    k += PIECES
    far_copy = copy(out_ref.at[far], far_in, k, at(2 * ahead))
    near_copy = copy(out_ref.at[back_near], near_in, k + 1, partner)
    k += 2
    weights = []
    for i, bit in enumerate(bits):
        src = wpart_ref if i == 0 else wsum.at[i - 1]
        weights.append(copy(src, wsum_in.at[i], k + i, across(bit)))
    weights[0].start()
    for one in helps:
        one.start()
    far_copy.start()
    near_copy.start()
    for p, c in enumerate(cuts):
        helps[p].wait_recv()
        both[c] = (
            out_ref[near, c].astype(jnp.float32) + far_here[c].astype(jnp.float32)
        ).astype(jnp.bfloat16)
        summed[p].start()
    for i in range(len(bits)):
        weights[i].wait_recv()
        total = (wpart_ref[...] if i == 0 else wsum[i - 1]) + wsum_in[i]
        if i + 1 < len(bits):
            wsum[i] = total
            weights[i + 1].start()
        else:
            wg_ref[...] = total * scale
    near_copy.wait_recv()
    far_copy.wait_recv()
    for p, c in enumerate(cuts):
        summed[p].wait_recv()
        ig_ref[c] = (
            mid_ref[c]
            + near_in[c].astype(jnp.float32)
            + far_in[c].astype(jnp.float32)
            + both_in[c].astype(jnp.float32)
        ).astype(jnp.bfloat16)
    for one in helps + summed + weights + [far_copy, near_copy]:
        one.wait_send()


def on_device(cotangent, relu_mask, aggregated, weight, tiles, col_block, live_count):
    blocks, cols, size = cotangent.shape
    slots = tiles.shape[1]
    slabs, reps = lax.axis_size("blk"), lax.axis_size("rep")
    width = weight.shape[1]
    ring = reps // 2
    bf16, f32 = jnp.bfloat16, jnp.float32
    dma = pltpu.SemaphoreType.DMA

    grad_h, wpart, tiles_here = pl.pallas_call(
        functools.partial(gather_kernel, ring),
        out_shape=(
            jax.ShapeDtypeStruct((blocks, cols, size), bf16),
            jax.ShapeDtypeStruct((cols, width), f32),
            jax.ShapeDtypeStruct(tiles.shape, bf16),
        ),
        in_specs=[HBM] * 5,
        out_specs=(VMEM, VMEM, VMEM),
        scratch_shapes=[
            pltpu.VMEM((blocks, cols, size), bf16),
            pltpu.VMEM((blocks, cols, size), jnp.int32),
            pltpu.VMEM((blocks, cols, size), bf16),
            pltpu.VMEM((cols, width), bf16),
            pltpu.VMEM((blocks, width, size), bf16),
            pltpu.VMEM((cols, width), f32),
            dma((5,)),
            dma((GROUPS, 7)),
            dma((GROUPS, reps)),
        ],
        compiler_params=pltpu.CompilerParams(
            collective_id=0, has_side_effects=True, vmem_limit_bytes=32 << 20
        ),
        name="gather",
    )(*[pltpu.with_memory_space_constraint(a, pltpu.HBM) for a in (cotangent, relu_mask, aggregated, weight)], tiles)

    middle, outer = pl.pallas_call(
        functools.partial(tile_kernel, slabs, blocks),
        out_shape=(
            jax.ShapeDtypeStruct((blocks, cols, size), f32),
            jax.ShapeDtypeStruct((2 * REACH, blocks, cols, size), bf16),
        ),
        in_specs=[SMEM, SMEM, VMEM, VMEM],
        out_specs=(VMEM, VMEM),
        scratch_shapes=[
            pltpu.VMEM(((2 * REACH + 1) * blocks + 1, cols, size), f32),
            pltpu.VMEM((slots, cols, size), f32),
            pltpu.SMEM((slots,), jnp.int32),
        ],
        compiler_params=pltpu.CompilerParams(vmem_limit_bytes=12 << 20),
        name="tiles",
    )(col_block.T, live_count, grad_h, tiles_here)

    scale = 1.0 / math.sqrt(slabs * blocks * size)
    levels = slabs.bit_length() - 1
    held = pltpu.VMEM((blocks, cols, size), bf16)
    count = 2 * PIECES + 2 + levels
    return pl.pallas_call(
        functools.partial(exchange_kernel, slabs, scale),
        out_shape=(
            jax.ShapeDtypeStruct((blocks, cols, size), bf16),
            jax.ShapeDtypeStruct((cols, width), f32),
        ),
        in_specs=[VMEM] * 3,
        out_specs=(VMEM, VMEM),
        scratch_shapes=[
            held, held, held, held, held,
            pltpu.VMEM((levels, cols, width), f32),
            pltpu.VMEM((levels, cols, width), f32),
            dma((count,)),
            dma((count,)),
        ],
        compiler_params=pltpu.CompilerParams(
            collective_id=1, has_side_effects=True, vmem_limit_bytes=32 << 20
        ),
        name="exchange",
    )(middle, outer, wpart)


def solution(mesh):
    placed = (
        P("blk", "rep", None),
        P("blk", "rep", None),
        P("blk", "rep", None),
        P("rep", None),
        P("blk", None, None, None),
        P("blk", None),
        P("blk"),
    )
    return jax.shard_map(
        on_device,
        mesh=mesh,
        in_specs=placed,
        out_specs=(P("blk", "rep", None), P("rep", None)),
        check_vma=False,
    )
```
